128 devices in a mesh: row: 32 (over y, z, core), col: 4 (over x).
Axes of the slice: x: 4, y: 4, z: 4, core: 2. Of those that a mesh axis runs over, the one named last changes fastest.
Arguments:
- matrix: float32 [16384, 16, 512], P('row', 'col'), may hold values from -200 to 200, as said below
Outputs:
- factored: float32 [16384, 16, 512], P('row', 'col')
- upper_rows: float32 [2, 512, 16, 512], P(None, 'row', 'col')
The draws below stay inside these ranges and needn't reach their ends.
Inputs may be any that keep to these rules, and one draw needn't show every extreme that they name: `matrix`: Real-valued entries; every panel has full column rank.
All inputs are finite; a program needn't handle non-finite values.
Results may differ from the reference program's by a relative error of at most 0.0001.
Values sent between devices are 32-bit elements; how exact they have to be, the bound alone decides.
A program may use at most 128 MiB of HBM per device.

```python
import jax
import jax.numpy as jnp
from jax import lax

PW = 512
BLK_DEV = 4
PANELS = 2
ROWS = 16384
NB = 16
N_COL = 4


def draw_matrix(key, part):
    keys = jax.random.split(jax.random.fold_in(key, 17), 3)
    base = jnp.clip(jax.random.normal(keys[0], (ROWS, NB, PW), jnp.float32), -6.0, 6.0)
    row_scale = jnp.exp(jax.random.uniform(keys[1], (ROWS, 1, 1), jnp.float32) * jnp.log(2.0))
    col_scale = jnp.exp(jax.random.uniform(keys[2], (1, NB, PW), jnp.float32) * jnp.log(4.0))
    return base * row_scale * col_scale


def setup_inputs(seed: int = 0) -> dict:
    streams_of = jax.random.split(jax.random.key(seed), 2)
    return {
        "matrix": draw_matrix(jax.random.fold_in(streams_of[1], 71), 0),
    }


HIGH = lax.Precision.HIGHEST

def right_solve(lower, block):
    return lax.linalg.triangular_solve(lower, block, left_side=False, lower=True, transpose_a=True)

def factor_panel(panel):
    half = panel.shape[1] // 2
    first = panel[:, :half]
    second = panel[:, half:]
    gram_one = jnp.dot(first.T, first, precision=HIGH)
    lower_one = jnp.linalg.cholesky(gram_one)
    basis_one = right_solve(lower_one, first)
    inner = jnp.dot(basis_one.T, second, precision=HIGH)
    rest = second - jnp.dot(basis_one, inner, precision=HIGH)
    gram_two = jnp.dot(rest.T, rest, precision=HIGH)
    lower_two = jnp.linalg.cholesky(gram_two)
    basis_two = right_solve(lower_two, rest)
    basis = jnp.concatenate([basis_one, basis_two], axis=1)
    top = jnp.concatenate([lower_one.T, inner], axis=1)
    bottom = jnp.concatenate([jnp.zeros((half, half), jnp.float32), lower_two.T], axis=1)
    return (basis, jnp.concatenate([top, bottom], axis=0))

def reference(matrix):
    work = matrix
    scale = jnp.sqrt(jnp.float32(ROWS))
    stored = jnp.arange(NB)
    number = stored % BLK_DEV * N_COL + stored // BLK_DEV
    pieces = []
    for k in range(PANELS):
        place = k % N_COL * BLK_DEV + k // N_COL
        basis, upper = factor_panel(work[:, place, :])
        keep = (number > k).astype(jnp.float32)
        weights = jnp.einsum('rk,rbc->kbc', basis, work, precision=HIGH) * keep[None, :, None]
        work = work - jnp.einsum('rk,kbc->rbc', basis, weights, precision=HIGH)
        work = work.at[:, place, :].set(basis * scale)
        pieces.append(weights.at[:, place, :].set(upper))
    return (work, jnp.stack(pieces, axis=0))
```

```python
import jax
import jax.numpy as jnp
from jax import lax
from jax.sharding import PartitionSpec as P

PANELS = 2
HIGHEST = lax.Precision.HIGHEST
HIGH = lax.Precision.HIGH


def spread(value, axis, root):
    mine = lax.axis_index(axis) == root
    return lax.psum(jnp.where(mine, value, jnp.zeros_like(value)), axis)


def on_device(matrix):
    work = matrix
    row_dev, blocks, width = matrix.shape
    n_row = lax.axis_size("row")
    n_col = lax.axis_size("col")
    my_col = lax.axis_index("col")
    my_row = lax.axis_index("row")
    share = width // n_row
    scale = jnp.sqrt(jnp.float32(row_dev * n_row))
    number = jnp.arange(blocks) * n_col + my_col
    pieces = []
    for k in range(PANELS):
        root = k % n_col
        slot = k // n_col
        owner = my_col == root
        panel = spread(work[:, slot, :], "col", root)
        keep = (number > k).astype(jnp.float32)
        gram = jnp.dot(panel.T, panel, precision=HIGHEST)
        terms = jnp.einsum("rk,rbc->kbc", panel, work, precision=HIGH) * keep[None, :, None]
        both = lax.psum(jnp.concatenate([gram[:, None, :], terms], axis=1), "row")
        gram, terms = both[:, 0, :], both[:, 1:, :]
        lower = jnp.linalg.cholesky(gram)
        eye = jnp.eye(width, dtype=jnp.float32)
        inverse = lax.linalg.triangular_solve(lower, eye, left_side=True, lower=True)
        basis = jnp.dot(panel, inverse.T, precision=HIGHEST)
        weights = jnp.einsum("ij,jbc->ibc", inverse, terms, precision=HIGH)
        work = work - jnp.einsum("rk,kbc->rbc", basis, weights, precision=HIGH)
        work = work.at[:, slot, :].set(jnp.where(owner, basis * scale, work[:, slot, :]))
        mine = lax.dynamic_slice_in_dim(weights, my_row * share, share, 0)
        upper_share = lax.dynamic_slice_in_dim(lower.T, my_row * share, share, 0)
        mine = mine.at[:, slot, :].set(jnp.where(owner, upper_share, mine[:, slot, :]))
        pieces.append(mine)
    return (work, jnp.stack(pieces, axis=0))


def solution(mesh):
    placed = (P("row", "col", None),)
    return jax.shard_map(
        on_device,
        mesh=mesh,
        in_specs=placed,
        out_specs=(P("row", "col", None), P(None, "row", "col", None)),
        check_vma=False,
    )
```

```python
import functools

import jax
import jax.numpy as jnp
from jax import lax
from jax.experimental import pallas as pl
from jax.experimental.pallas import tpu as pltpu
from jax.sharding import PartitionSpec as P

PANELS = 2
W = 512
SLOTS = 4
NZ = 4
NY = 4
NX = 4
PIECES = 4
HIGHEST = lax.Precision.HIGHEST
MESH = pl.DeviceIdType.MESH
F32 = jnp.float32
VMEM = pl.BlockSpec(memory_space=pltpu.VMEM)
ANY = pl.BlockSpec(memory_space=pl.ANY)


def here():
    row = lax.axis_index("row")
    x = lax.axis_index("col")
    return x, lax.div(row, 2 * NZ), lax.rem(lax.div(row, 2), NZ), lax.rem(row, 2)


def device(dx=0, dy=0, dz=0, dc=0):
    x, y, z, c = here()
    x, y, z, c = lax.rem(x + dx, NX), lax.rem(y + dy, NY), lax.rem(z + dz, NZ), lax.rem(c + dc, 2)
    return ((y * NZ + z) * 2 + c, x)


def rows(start, size):
    return pl.ds(pl.multiple_of(start, 8), size)


def meet(peers):
    barrier = pltpu.get_barrier_semaphore()
    for peer in peers:
        pl.semaphore_signal(barrier, inc=1, device_id=peer, device_id_type=MESH)
    pl.semaphore_wait(barrier, len(peers))


def plane_peers():
    return (
        [device(dc=1)]
        + [device(dz=d) for d in range(1, NZ)]
        + [device(dy=d) for d in range(1, NY)]
    )


class Copies:
    def __init__(self, send, recv):
        self.send, self.recv, self.used = send, recv, 0

    def make(self, src, dst, peer):
        i = self.used
        self.used += 1
        return pltpu.make_async_remote_copy(
            src_ref=src, dst_ref=dst, send_sem=self.send.at[i], recv_sem=self.recv.at[i],
            device_id=peer, device_id_type=MESH,
        )

    def start(self, src, dst, peer):
        copy = self.make(src, dst, peer)
        copy.start()
        return copy


def split(value):
    high = value.astype(jnp.bfloat16)
    return high, (value - high.astype(F32)).astype(jnp.bfloat16)


def dot3(a, b, dims):
    dg = functools.partial(
        lax.dot_general, dimension_numbers=(dims, ((), ())), preferred_element_type=F32
    )
    return dg(a[0], b[0]) + (dg(a[0], b[1]) + dg(a[1], b[0]))


def dot6(a, b, dims):
    return lax.dot_general(a, b, (dims, ((), ())), precision=HIGHEST, preferred_element_type=F32)


OVER_ROWS = ((0,), (0,))
OVER_COLS = ((1,), (1,))
PLAIN = ((1,), (0,))


def leaf_inverse(slabs):
    n = len(slabs)
    w = 8 * n
    lane = lax.broadcasted_iota(jnp.int32, (8, w), 1)
    sub = lax.broadcasted_iota(jnp.int32, (8, w), 0)
    slabs = list(slabs)
    for b in range(n):
        r = slabs[b]
        inside = (lane >= 8 * b) & (lane < 8 * b + 8)
        cols = [jnp.broadcast_to(r[:, 8 * b + s : 8 * b + s + 1], (8, w)) for s in range(8)]
        d = [[jnp.broadcast_to(cols[s][t : t + 1, :], (8, w)) for s in range(t + 1)] for t in range(8)]
        r = jnp.where(inside, jnp.where(lane == 8 * b + sub, 1.0, 0.0), r)
        line = [jnp.broadcast_to(r[s : s + 1, :], (8, w)) for s in range(8)]
        rp = [None] * 8
        m = {}
        for s in range(8):
            rp[s] = 1.0 / d[s][s]
            for t in range(s + 1, 8):
                m[t, s] = d[t][s] * rp[s]
            for t in range(s + 1, 8):
                for u in range(s + 1, t + 1):
                    d[t][u] = d[t][u] - m[t, s] * d[u][s]
                line[t] = line[t] - m[t, s] * line[s]
        out, pivot = line[0], d[0][0]
        for s in range(1, 8):
            out = jnp.where(sub == s, line[s], out)
            pivot = jnp.where(sub == s, d[s][s], pivot)
        slabs[b] = out * (1.0 / jnp.sqrt(pivot))
        if b < n - 1:
            z = [None] * 8
            for s in reversed(range(8)):
                z[s] = line[s] * rp[s]
                for t in range(s + 1, 8):
                    z[s] = z[s] - m[t, s] * z[t]
            for i in range(b + 1, n):
                e = slabs[i]
                acc = jnp.where(inside, 0.0, e)
                for s in range(8):
                    acc = acc - jnp.broadcast_to(e[:, 8 * b + s : 8 * b + s + 1], (8, w)) * z[s]
                slabs[i] = acc
    return slabs


def factor(z_ref, u_ref):
    w = 128
    ri = lax.broadcasted_iota(jnp.int32, (w, w), 0)
    ci = lax.broadcasted_iota(jnp.int32, (w, w), 1)
    wide = lax.broadcasted_iota(jnp.int32, (w, W), 1)
    down = lax.broadcasted_iota(jnp.int32, (w, W), 0)

    @pl.loop(0, W // w)
    def _(j):
        here = pl.ds(pl.multiple_of(j * w, w), w)
        block = z_ref[here, here]
        y = jnp.concatenate(leaf_inverse([block[8 * i : 8 * i + 8] for i in range(w // 8)]), axis=0)
        y = jnp.where(ci <= ri, y, 0.0)
        t = dot6(y, z_ref[here, :], PLAIN)
        u_ref[here, :] = jnp.where(wide >= j * w + down, t, 0.0)
        z_ref[here, :] = t
        z_ref[here, here] = y

        @pl.loop(j + 1, W // w)
        def _(i):
            there = pl.ds(pl.multiple_of(i * w, w), w)
            z_ref[there, here] = jnp.zeros((w, w), F32)
            z_ref[there, :] = z_ref[there, :] - dot6(u_ref[here, there], z_ref[here, :], OVER_ROWS)

    @pl.loop(0, W // w)
    def _(j):
        here = pl.ds(pl.multiple_of(j * w, w), w)
        z_ref[here, :] = jnp.where(wide <= j * w + down, z_ref[here, :], 0.0)


def factor_kernel(g_ref, z_ref, u_ref):
    z_ref[...] = g_ref[...]
    factor(z_ref, u_ref)


def gather_kernel(k, x_ref, p_out, g_out, h_out, xs, pv, g, h, g0, g1, g2, h0, h1, h2, send, recv, local):
    x, y, z, c = here()
    other = 1 - c
    d = lax.rem(x - k % NX + NX, NX)
    copies = Copies(send, recv)
    slot = (lambda j: x_ref.at[:, j, :]) if k == 0 else (lambda j: x_ref.at[j])
    loads = [pltpu.make_async_copy(slot(j), xs.at[j], local.at[j]) for j in range(SLOTS)]
    seed = pltpu.make_async_copy(slot(0), pv, local.at[SLOTS])

    @pl.when(d == 0)
    def _():
        seed.start()

    for load in loads:
        load.start()
    meet(plane_peers() + [device(dx=1), device(dx=NX - 1)])

    @pl.when(d == 0)
    def _():
        seed.wait()

    half = W // 2
    step = half // PIECES
    right = [copies.make(pv.at[pl.ds(i * step, step)], pv.at[pl.ds(i * step, step)], device(dx=1)) for i in range(PIECES)]
    left = [
        copies.make(pv.at[pl.ds(half + i * step, step)], pv.at[pl.ds(half + i * step, step)], device(dx=NX - 1))
        for i in range(PIECES)
    ]
    @pl.when(d == 0)
    def _():
        for a, b in zip(right, left):
            a.start()
            b.start()

    @pl.when(d == 1)
    def _():
        for a in right:
            a.wait_recv()
            a.start()
        for b in left:
            b.wait_recv()

    @pl.when(d == 2)
    def _():
        for a, b in zip(right, left):
            a.wait_recv()
            a.start()
            b.wait_recv()
            b.start()

    @pl.when(d == NX - 1)
    def _():
        for b in left:
            b.wait_recv()
            b.start()
        for a in right:
            a.wait_recv()

    panel = pv[...]
    ph = split(panel)
    g[...] = dot6(panel, panel, OVER_ROWS)

    def term(j):
        h[j] = dot3(split(xs[j]), ph, OVER_ROWS)

    eighth = W // 8
    gs = []
    s0 = copies.start(g.at[rows(other * half, half)], g0, device(dc=1))
    for load in loads:
        load.wait()
    hs0 = []
    for i in range(2):
        term(other * 2 + i)
        hs0.append(copies.start(h.at[other * 2 + i], h0.at[i], device(dc=1)))

    def spread_out(buf, at, size, into, axis, me, n):
        started = []
        for e in range(1, n):
            to = lax.rem(me + e, n)
            started.append(copies.start(buf.at[rows(at + to * size, size)], into.at[e - 1], device(**{axis: e})))
        return started

    def collect(buf, at, size, into, me, started):
        for copy in started:
            copy.wait_recv()
        mine = rows(at + me * size, size)
        buf[mine] = buf[mine] + ((into[0] + into[1]) + into[2])
        return at + me * size

    def reduce_two(a_buf, a_at, b_buf, b_at, size, first, second):
        sa = spread_out(a_buf, a_at, size, first.at[0], "dz", z, NZ)
        sb = spread_out(b_buf, b_at, size, first.at[1], "dy", y, NY)
        a_at = collect(a_buf, a_at, size, first.at[0], z, sa)
        b_at = collect(b_buf, b_at, size, first.at[1], y, sb)
        ta = spread_out(a_buf, a_at, size // 4, second.at[0], "dy", y, NY)
        tb = spread_out(b_buf, b_at, size // 4, second.at[1], "dz", z, NZ)
        a_at = collect(a_buf, a_at, size // 4, second.at[0], y, ta)
        b_at = collect(b_buf, b_at, size // 4, second.at[1], z, tb)
        return a_at, b_at, sa + sb + ta + tb

    def share(buf, at, size, axis, n):
        return [copies.start(buf.at[rows(at, size)], buf.at[rows(at, size)], device(**{axis: e})) for e in range(1, n)]

    s0.wait_recv()
    own = rows(c * half, half)
    g[own] = g[own] + g0[...]
    q = half // 2
    a0, b0 = c * half, c * half + q
    a_at, b_at, more = reduce_two(g, a0, g, b0, q // 4, g1, g2)
    gs += [s0] + more
    gf = g_out
    for at in (a_at, b_at):
        gf[rows(at, q // 16)] = g[rows(at, q // 16)]
    a = share(gf, a_at, q // 16, "dy", NY)
    b = share(gf, b_at, q // 16, "dz", NZ)
    for copy in a + b:
        copy.wait_recv()
    gs += a + b
    a = share(gf, a0 + z * (q // 4), q // 4, "dz", NZ)
    b = share(gf, b0 + y * (q // 4), q // 4, "dy", NY)
    for copy in a + b:
        copy.wait_recv()
    gs += a + b
    last = copies.start(gf.at[own], gf.at[own], device(dc=1))

    for i in range(2):
        term(c * 2 + i)
    for i in range(2):
        hs0[i].wait_recv()
        h[c * 2 + i] = h[c * 2 + i] + h0[i]
    a_at, b_at, more = reduce_two(h.at[c * 2], 0, h.at[c * 2 + 1], 0, W // 4, h1, h2)
    h_out[0] = h[c * 2, rows(a_at, 32)]
    h_out[1] = h[c * 2 + 1, rows(b_at, 32)]
    last.wait_recv()
    p_out[...] = panel
    for copy in gs + [last] + hs0 + more:
        copy.wait_send()
    for a, b in zip(right, left):
        @pl.when(d != NX - 1)
        def _():
            a.wait_send()

        @pl.when(d != 1)
        def _():
            b.wait_send()


def update_kernel(k, scale, x_ref, p_ref, z_ref, u_ref, h_ref, x_out, r_out, xs, wt, up, send, recv, local):
    x, y, z, c = here()
    copies = Copies(send, recv)
    source = (lambda j: x_ref.at[:, j, :]) if k == 0 else (lambda j: x_ref.at[j])
    target = (lambda j: x_out.at[:, j, :]) if k == PANELS - 1 else (lambda j: x_out.at[j])
    loads = [pltpu.make_async_copy(source(j), xs.at[j], local.at[j]) for j in range(SLOTS)]
    for load in loads:
        load.start()
    meet(plane_peers())
    sa, sb = c * 2, c * 2 + 1
    zi = z_ref[...]
    wt[sa, rows(z * 128 + y * 32, 32)] = dot6(h_ref[0], zi, OVER_COLS)
    wt[sb, rows(y * 128 + z * 32, 32)] = dot6(h_ref[1], zi, OVER_COLS)

    def share(j, at, size, peer):
        ref = wt.at[j, rows(at, size)]
        return copies.start(ref, ref, peer)

    s1 = [share(sa, z * 128 + y * 32, 32, device(dy=e)) for e in range(1, NY)]
    s1 += [share(sb, y * 128 + z * 32, 32, device(dz=e)) for e in range(1, NZ)]
    basis = dot6(p_ref[...], zi, OVER_COLS)
    qh = split(basis)
    for copy in s1:
        copy.wait_recv()
    s2a = [share(sa, z * 128, 128, device(dz=e)) for e in range(1, NZ)]
    s2b = [share(sb, y * 128, 128, device(dy=e)) for e in range(1, NY)]
    s3 = [share(sa, z * 128, 128, device(dc=1)), share(sb, y * 128, 128, device(dc=1))]
    for e in range(1, NZ):
        s2a[e - 1].wait_recv()
        s3.append(share(sa, lax.rem(z + NZ - e, NZ) * 128, 128, device(dc=1)))
        s2b[e - 1].wait_recv()
        s3.append(share(sb, lax.rem(y + NY - e, NY) * 128, 128, device(dc=1)))
    for load in loads:
        load.wait()
    row = (y * NZ + z) * 2 + c
    pick = jnp.where(
        lax.broadcasted_iota(jnp.int32, (16, W), 1) == row * 16 + lax.broadcasted_iota(jnp.int32, (16, W), 0), 1.0, 0.0
    ).astype(F32)

    def apply(j):
        w = wt[j]
        new = xs[j] - dot3(qh, split(w), OVER_COLS)
        line = dot6(pick, w, OVER_COLS)
        first = j == 0
        new = jnp.where(first & (x < k), xs[j], jnp.where(first & (x == k), basis * scale, new))
        line = jnp.where(first & (x < k), 0.0, jnp.where(first & (x == k), u_ref[rows(row * 16, 16)], line))
        xs[j] = new
        up[j] = line
        stores = [
            pltpu.make_async_copy(xs.at[j], target(j), local.at[SLOTS + j]),
            pltpu.make_async_copy(up.at[j], r_out.at[:, j, :], local.at[2 * SLOTS + j]),
        ]
        for store in stores:
            store.start()
        return stores

    stores = apply(sa) + apply(sb)
    for copy in s3:
        copy.wait_recv()
    stores += apply((1 - c) * 2) + apply((1 - c) * 2 + 1)
    for store in stores:
        store.wait()
    for copy in s1 + s2a + s2b + s3:
        copy.wait_send()


def params(cid=None):
    if cid is None:
        return pltpu.CompilerParams(vmem_limit_bytes=48 * 2**20)
    return pltpu.CompilerParams(collective_id=cid, has_side_effects=True, vmem_limit_bytes=60 * 2**20)


def shape(*dims):
    return jax.ShapeDtypeStruct(dims, F32)


def on_device(matrix):
    work = matrix
    n = matrix.shape[0]
    scale = float(n * lax.axis_size("row")) ** 0.5
    dma = pltpu.SemaphoreType.DMA
    pieces = []
    for k in range(PANELS):
        panel, gram, terms = pl.pallas_call(
            functools.partial(gather_kernel, k),
            out_shape=(shape(W, W), shape(W, W), shape(2, 32, W)),
            in_specs=[ANY],
            out_specs=(VMEM, VMEM, VMEM),
            scratch_shapes=[
                pltpu.VMEM((SLOTS, n, W), F32), pltpu.VMEM((n, W), F32), pltpu.VMEM((W, W), F32),
                pltpu.VMEM((SLOTS, W, W), F32),
                pltpu.VMEM((W // 2, W), F32), pltpu.VMEM((2, 3, 32, W), F32), pltpu.VMEM((2, 3, 8, W), F32),
                pltpu.VMEM((2, W, W), F32), pltpu.VMEM((2, 3, 128, W), F32), pltpu.VMEM((2, 3, 32, W), F32),
                dma((64,)), dma((64,)), dma((8,)),
            ],
            compiler_params=params(1 + 2 * k),
            name=f"gather_{k}",
        )(work)
        inverse, upper = pl.pallas_call(
            factor_kernel, out_shape=(shape(W, W), shape(W, W)), in_specs=[VMEM], out_specs=(VMEM, VMEM),
            compiler_params=params(), name=f"factor_{k}",
        )(gram)
        last = k == PANELS - 1
        work, mine = pl.pallas_call(
            functools.partial(update_kernel, k, scale),
            out_shape=(shape(n, SLOTS, W) if last else shape(SLOTS, n, W), shape(W // 32, SLOTS, W)),
            in_specs=[ANY, VMEM, VMEM, VMEM, VMEM],
            out_specs=(ANY, ANY),
            scratch_shapes=[
                pltpu.VMEM((SLOTS, n, W), F32), pltpu.VMEM((SLOTS, W, W), F32), pltpu.VMEM((SLOTS, W // 32, W), F32),
                dma((32,)), dma((32,)), dma((16,)),
            ],
            compiler_params=params(2 + 2 * k),
            name=f"update_{k}",
        )(work, panel, inverse, upper, terms)
        pieces.append(mine)
    return (work, jnp.stack(pieces, axis=0))


def solution(mesh):
    return jax.shard_map(
        on_device,
        mesh=mesh,
        in_specs=(P("row", "col", None),),
        out_specs=(P("row", "col", None), P(None, "row", "col", None)),
        check_vma=False,
    )
```

```python
import functools

import jax
import jax.numpy as jnp
from jax import lax
from jax.experimental import pallas as pl
from jax.experimental.pallas import tpu as pltpu
from jax.sharding import PartitionSpec as P

PANELS = 2
W = 512
SLOTS = 4
NZ = 4
NY = 4
NX = 4
PIECES = 4
LEAF = 128
HIGHEST = lax.Precision.HIGHEST
MESH = pl.DeviceIdType.MESH
F32 = jnp.float32
ANY = pl.BlockSpec(memory_space=pl.ANY)


def here():
    row = lax.axis_index("row")
    x = lax.axis_index("col")
    return x, lax.div(row, 2 * NZ), lax.rem(lax.div(row, 2), NZ), lax.rem(row, 2)


def device(dx=0, dy=0, dz=0, dc=0):
    x, y, z, c = here()
    x, y, z, c = lax.rem(x + dx, NX), lax.rem(y + dy, NY), lax.rem(z + dz, NZ), lax.rem(c + dc, 2)
    return ((y * NZ + z) * 2 + c, x)


def rows(start, size):
    return pl.ds(pl.multiple_of(start, 8), size)


def meet(peers):
    barrier = pltpu.get_barrier_semaphore()
    for peer in peers:
        pl.semaphore_signal(barrier, inc=1, device_id=peer, device_id_type=MESH)
    pl.semaphore_wait(barrier, len(peers))


class Copies:
    def __init__(self, send, recv):
        self.send, self.recv, self.used = send, recv, 0

    def make(self, src, dst, peer):
        i = self.used
        self.used += 1
        return pltpu.make_async_remote_copy(
            src_ref=src, dst_ref=dst, send_sem=self.send.at[i], recv_sem=self.recv.at[i],
            device_id=peer, device_id_type=MESH,
        )


def start(copies):
    for copy in copies:
        copy.start()


def arrive(copies):
    for copy in copies:
        copy.wait_recv()


def drain(copies):
    for copy in copies:
        copy.wait_send()


def to_others(make, buf, at, size, into, axis, me, n):
    return [
        make(buf.at[rows(at + lax.rem(me + e, n) * size, size)], into.at[e - 1], device(**{axis: e})) for e in range(1, n)
    ]


def to_all(make, buf, at, size, axis, n):
    return [make(buf.at[rows(at, size)], buf.at[rows(at, size)], device(**{axis: e})) for e in range(1, n)]


class Reduce:
    def __init__(self, make, a_buf, a_at, b_buf, b_at, size, first, second):
        x, y, z, c = here()
        q = size // 4
        self.parts = []
        for i, (buf, at, one, two) in enumerate(((a_buf, a_at, ("dz", z), ("dy", y)), (b_buf, b_at, ("dy", y), ("dz", z)))):
            mid = at + one[1] * size
            end = mid + two[1] * q
            s1 = to_others(make, buf, at, size, first.at[i], one[0], one[1], 4)
            s2 = to_others(make, buf, mid, q, second.at[i], two[0], two[1], 4)
            self.parts.append((buf, mid, size, first.at[i], s1, end, q, second.at[i], s2))

    def begin(self):
        for p in self.parts:
            start(p[4])

    def middle(self):
        for buf, mid, size, into, s1, end, q, into2, s2 in self.parts:
            arrive(s1)
            buf[rows(mid, size)] = buf[rows(mid, size)] + ((into[0] + into[1]) + into[2])
            start(s2)

    def finish(self):
        for buf, mid, size, into, s1, end, q, into2, s2 in self.parts:
            arrive(s2)
            buf[rows(end, q)] = buf[rows(end, q)] + ((into2[0] + into2[1]) + into2[2])

    def drain(self):
        for p in self.parts:
            drain(p[4])
            drain(p[8])


class AllReduce:
    def __init__(self, make, g, out, g0, g1, g2):
        x, y, z, c = here()
        half = W // 2
        q = half // 2
        a0, b0 = c * half, c * half + q
        self.g, self.out, self.g0 = g, out, g0
        self.own = rows(c * half, half)
        self.core = make(g.at[rows((1 - c) * half, half)], g0, device(dc=1))
        self.red = Reduce(make, g, a0, g, b0, q // 4, g1, g2)
        self.ends = [(p[5], p[6]) for p in self.red.parts]
        self.s1 = to_all(make, out, self.ends[0][0], q // 16, "dy", NY) + to_all(make, out, self.ends[1][0], q // 16, "dz", NZ)
        self.s2 = to_all(make, out, a0 + z * (q // 4), q // 4, "dz", NZ) + to_all(make, out, b0 + y * (q // 4), q // 4, "dy", NY)
        self.last = make(out.at[self.own], out.at[self.own], device(dc=1))

    def step(self, i):
        if i == 0:
            self.core.start()
        elif i == 1:
            self.core.wait_recv()
            self.g[self.own] = self.g[self.own] + self.g0[...]
            self.red.begin()
        elif i == 2:
            self.red.middle()
        elif i == 3:
            self.red.finish()
            for at, q in self.ends:
                self.out[rows(at, q)] = self.g[rows(at, q)]
            start(self.s1)
        elif i == 4:
            arrive(self.s1)
            start(self.s2)
        elif i == 5:
            arrive(self.s2)
            self.last.start()
        else:
            self.last.wait_recv()

    def drain(self):
        self.red.drain()
        drain([self.core, self.last] + self.s1 + self.s2)


class Scatter:
    def __init__(self, make, h, h0, h1, h2):
        x, y, z, c = here()
        self.h, self.h0, self.c = h, h0, c
        self.core = [make(h.at[(1 - c) * 2 + i], h0.at[i], device(dc=1)) for i in range(2)]
        self.red = Reduce(make, h.at[c * 2], 0, h.at[c * 2 + 1], 0, W // 4, h1, h2)

    def add(self, i):
        self.core[i].wait_recv()
        self.h[self.c * 2 + i] = self.h[self.c * 2 + i] + self.h0[i]

    def part(self, i):
        p = self.red.parts[i]
        return p[0][rows(p[5], p[6])]

    def drain(self):
        self.red.drain()
        drain(self.core)


class Gather:
    def __init__(self, make, wt):
        x, y, z, c = here()
        self.wt = wt
        a, b = wt.at[c * 2], wt.at[c * 2 + 1]
        self.at = ((c * 2, z * 128 + y * 32), (c * 2 + 1, y * 128 + z * 32))
        self.s1 = to_all(make, a, z * 128 + y * 32, 32, "dy", NY) + to_all(make, b, y * 128 + z * 32, 32, "dz", NZ)
        self.s2a = to_all(make, a, z * 128, 128, "dz", NZ)
        self.s2b = to_all(make, b, y * 128, 128, "dy", NY)
        self.s3a = [self.pair(make, a, lax.rem(z + NZ - e, NZ) * 128) for e in range(NZ)]
        self.s3b = [self.pair(make, b, lax.rem(y + NY - e, NY) * 128) for e in range(NY)]

    def pair(self, make, buf, at):
        return make(buf.at[rows(at, 128)], buf.at[rows(at, 128)], device(dc=1))

    def begin(self):
        start(self.s1)

    def middle(self):
        arrive(self.s1)
        start(self.s2a)
        start(self.s2b)
        start([self.s3a[0], self.s3b[0]])

    def forward(self):
        for e in range(1, NZ):
            arrive([self.s2a[e - 1]])
            start([self.s3a[e]])
            arrive([self.s2b[e - 1]])
            start([self.s3b[e]])

    def finish(self):
        arrive(self.s3a)
        arrive(self.s3b)

    def drain(self):
        drain(self.s1 + self.s2a + self.s2b + self.s3a + self.s3b)


class Relay:
    def __init__(self, make, buf, root):
        x, y, z, c = here()
        half = W // 2
        step = half // PIECES
        self.d = lax.rem(x - root + NX, NX)
        self.right = [make(buf.at[pl.ds(i * step, step)], buf.at[pl.ds(i * step, step)], device(dx=1)) for i in range(PIECES)]
        self.left = [
            make(buf.at[pl.ds(half + i * step, step)], buf.at[pl.ds(half + i * step, step)], device(dx=NX - 1))
            for i in range(PIECES)
        ]

    def begin(self):
        @pl.when(self.d == 0)
        def _():
            for a, b in zip(self.right, self.left):
                a.start()
                b.start()

    def hop(self, i):
        a, b = self.right[i], self.left[i]

        @pl.when((self.d == 1) | (self.d == 2))
        def _():
            a.wait_recv()
            a.start()

        @pl.when((self.d == 2) | (self.d == 3))
        def _():
            b.wait_recv()
            b.start()

    def finish(self):
        @pl.when(self.d == 1)
        def _():
            arrive(self.left)

        @pl.when(self.d == 3)
        def _():
            arrive(self.right)

    def drain(self):
        @pl.when(self.d != 3)
        def _():
            drain(self.right)

        @pl.when(self.d != 1)
        def _():
            drain(self.left)


def split(value):
    high = value.astype(jnp.bfloat16)
    return high, (value - high.astype(F32)).astype(jnp.bfloat16)


def dot3(a, b, dims):
    dg = functools.partial(
        lax.dot_general, dimension_numbers=(dims, ((), ())), preferred_element_type=F32
    )
    return dg(a[0], b[0]) + (dg(a[0], b[1]) + dg(a[1], b[0]))


def dot6(a, b, dims):
    return lax.dot_general(a, b, (dims, ((), ())), precision=HIGHEST, preferred_element_type=F32)


OVER_ROWS = ((0,), (0,))
OVER_COLS = ((1,), (1,))
PLAIN = ((1,), (0,))


def lanes_of(v, k):
    return jnp.broadcast_to(v[:, k : k + 1], v.shape)


def sublanes_of(v, k):
    return jnp.broadcast_to(v[k : k + 1, :], v.shape)


def leaf_inverse(slabs, zero):
    n = len(slabs)
    lane = lax.broadcasted_iota(jnp.int32, zero.shape, 1)
    sub = lax.broadcasted_iota(jnp.int32, zero.shape, 0)
    slabs = list(slabs)
    for b in range(n):
        r = slabs[b]
        inside = (lane >= 8 * b) & (lane < 8 * b + 8)
        cols = [lanes_of(r, 8 * b + s) + zero for s in range(8)]
        d = [[sublanes_of(cols[s], t) for s in range(t + 1)] for t in range(8)]
        r = jnp.where(inside, jnp.where(lane == 8 * b + sub, 1.0, 0.0), r)
        line = [sublanes_of(r, s) for s in range(8)]
        ahead = b + 1 < n
        if ahead:
            e = [lanes_of(slabs[b + 1], 8 * b + s) for s in range(8)]
            nxt = jnp.where(inside, 0.0, slabs[b + 1])
        rp = [None] * 8
        m = {}
        for s in range(8):
            rp[s] = 1.0 / d[s][s]
            if ahead:
                f = e[s] * rp[s]
                nxt = nxt - f * line[s]
                for u in range(s + 1, 8):
                    e[u] = e[u] - f * d[u][s]
            for t in range(s + 1, 8):
                m[t, s] = d[t][s] * rp[s]
            for t in range(s + 1, 8):
                for u in range(s + 1, t + 1):
                    d[t][u] = d[t][u] - m[t, s] * d[u][s]
                line[t] = line[t] - m[t, s] * line[s]
        out, pivot = line[0], d[0][0]
        for s in range(1, 8):
            out = jnp.where(sub == s, line[s], out)
            pivot = jnp.where(sub == s, d[s][s], pivot)
        slabs[b] = out * (1.0 / jnp.sqrt(pivot))
        if ahead:
            slabs[b + 1] = nxt
        if b + 2 < n:
            z = [None] * 8
            for s in reversed(range(8)):
                z[s] = line[s] * rp[s]
                for t in range(s + 1, 8):
                    z[s] = z[s] - m[t, s] * z[t]
            for i in range(b + 2, n):
                acc = jnp.where(inside, 0.0, slabs[i])
                for s in range(8):
                    acc = acc - lanes_of(slabs[i], 8 * b + s) * z[s]
                slabs[i] = acc
    return slabs


def factor(z_ref, u_ref, zero_ref, after):
    w = LEAF
    ri = lax.broadcasted_iota(jnp.int32, (w, w), 0)
    ci = lax.broadcasted_iota(jnp.int32, (w, w), 1)
    wide = lax.broadcasted_iota(jnp.int32, (w, W), 1)
    down = lax.broadcasted_iota(jnp.int32, (w, W), 0)

    @pl.loop(0, W // w)
    def _(j):
        here = pl.ds(pl.multiple_of(j * w, w), w)
        block = z_ref[here, here]
        y = jnp.concatenate(leaf_inverse([block[8 * i : 8 * i + 8] for i in range(w // 8)], zero_ref[...]), axis=0)
        y = jnp.where(ci <= ri, y, 0.0)
        t = dot6(y, z_ref[here, :], PLAIN)
        u_ref[here, :] = jnp.where(wide >= j * w + down, t, 0.0)
        z_ref[here, :] = t
        z_ref[here, here] = y

        @pl.loop(j + 1, W // w)
        def _(i):
            there = pl.ds(pl.multiple_of(i * w, w), w)
            z_ref[there, here] = jnp.zeros((w, w), F32)
            z_ref[there, :] = z_ref[there, :] - dot6(u_ref[here, there], z_ref[here, :], OVER_ROWS)

        for step, do in after.items():
            pl.when(j == step)(do)

    @pl.loop(0, W // w)
    def _(j):
        here = pl.ds(pl.multiple_of(j * w, w), w)
        z_ref[here, :] = jnp.where(wide <= j * w + down, z_ref[here, :], 0.0)


def kernel(scale, x_ref, x_out, r_out, xs, p0, p1, pn, q0, q1, w01, z0, z1, u0, u1, zero, g, gf, g0, g1, g2,
           h, h0, h1, h2, wt, up, fix, send, recv, local):
    x, y, z, c = here()
    make = Copies(send, recv).make
    other = 1 - c
    loads = [pltpu.make_async_copy(x_ref.at[:, j, :], xs.at[j], local.at[j]) for j in range(SLOTS)]
    seeds = [pltpu.make_async_copy(x_ref.at[:, 0, :], p, local.at[SLOTS]) for p in (p0, p1)]
    for k in range(PANELS):
        @pl.when(x == k)
        def _():
            seeds[k].start()
    start(loads)
    zero[...] = jnp.zeros_like(zero)
    relay = [Relay(make, p, k) for k, p in enumerate((p0, p1))]
    whole = [AllReduce(make, g.at[i], gf.at[i], g0.at[i], g1.at[i], g2.at[i]) for i in range(3)]
    scatter = [Scatter(make, h, h0.at[k], h1.at[k], h2.at[k]) for k in range(PANELS)]
    gather = [Gather(make, wt.at[k]) for k in range(PANELS)]
    meet(
        [device(dc=1)] + [device(dz=d) for d in range(1, NZ)] + [device(dy=d) for d in range(1, NY)]
        + [device(dx=1), device(dx=NX - 1)]
    )
    for k in range(PANELS):
        @pl.when(x == k)
        def _():
            seeds[k].wait()

    relay[0].begin()
    for i in range(PIECES):
        relay[0].hop(i)
    relay[0].finish()
    relay[1].begin()

    first = p0[...]
    ph = split(first)
    g[0] = dot6(first, first, OVER_ROWS)
    whole[0].step(0)
    for load in loads:
        load.wait()

    def term(k, parts, j):
        h[j] = dot3(split(xs[j]), parts, OVER_ROWS)

    order = (other * 2, other * 2 + 1, c * 2, c * 2 + 1)
    for i in range(4):
        term(0, ph, order[i])
        if i < 2:
            scatter[0].core[i].start()
        whole[0].step(i + 1)
        relay[1].hop(i)
    for i in range(2):
        scatter[0].add(i)
    whole[0].step(5)
    scatter[0].red.begin()
    relay[1].finish()
    g[1] = dot6(first, p1[...], OVER_ROWS)
    whole[1].step(0)
    whole[0].step(6)
    z0[...] = gf[0]

    def late():
        whole[1].step(3)
        scatter[0].red.middle()

    factor(z0, u0, zero, {0: lambda: whole[1].step(1), 1: lambda: whole[1].step(2), 2: late, 3: lambda: whole[1].step(4)})
    scatter[0].red.finish()
    inverse = z0[...]

    def shards(k, parts, inv):
        for i, (slot, at) in enumerate(gather[k].at):
            wt[k, slot, rows(at, 32)] = dot6(parts[i], inv, OVER_COLS)

    shards(0, [scatter[0].part(i) for i in range(2)], inverse)
    gather[0].begin()
    whole[1].step(5)
    basis = dot6(first, inverse, OVER_COLS)
    q0[...] = basis
    whole[1].step(6)
    w01[...] = dot6(inverse, gf[1], PLAIN)
    gather[0].middle()

    pn[...] = p1[...] - dot6(q0[...], w01[...], PLAIN)
    g[2] = dot6(pn[...], pn[...], OVER_ROWS)
    whole[2].step(0)
    scatter[0].drain()
    pf = split(p1[...])
    for i in range(4):
        term(1, pf, order[i])
        if i < 2:
            scatter[1].core[i].start()
        whole[2].step(i + 1)
    for i in range(2):
        scatter[1].add(i)
    whole[2].step(5)
    scatter[1].red.begin()
    gather[0].forward()
    for i, (slot, at) in enumerate(gather[0].at):
        fix[i] = dot6(wt[0, slot, rows(at, 32)], w01[...], PLAIN)
    whole[2].step(6)
    z1[...] = gf[2]
    factor(z1, u1, zero, {2: scatter[1].red.middle})
    scatter[1].red.finish()
    inverse = z1[...]
    shards(1, [scatter[1].part(i) - fix[i] for i in range(2)], inverse)
    gather[1].begin()
    q1[...] = dot6(pn[...], inverse, OVER_COLS)

    row = (y * NZ + z) * 2 + c
    mine = rows(row * 16, 16)
    pick = jnp.where(
        lax.broadcasted_iota(jnp.int32, (16, W), 1) == row * 16 + lax.broadcasted_iota(jnp.int32, (16, W), 0), 1.0, 0.0
    ).astype(F32)
    basis = (q0, q1)
    upper = (u0, u1)

    def apply(k, j):
        w = wt[k, j]
        new = xs[j] - dot3(split(basis[k][...]), split(w), OVER_COLS)
        line = dot6(pick, w, OVER_COLS)
        skip = (j == 0) & (x < k)
        owner = (j == 0) & (x == k)
        xs[j] = jnp.where(skip, xs[j], jnp.where(owner, basis[k][...] * scale, new))
        up[k, j] = jnp.where(skip, 0.0, jnp.where(owner, upper[k][mine], line))

    stores = []

    def put(j):
        stores.append(pltpu.make_async_copy(xs.at[j], x_out.at[:, j, :], local.at[SLOTS + 1 + j]))
        stores.append(pltpu.make_async_copy(up.at[:, j], r_out.at[:, :, j, :], local.at[2 * SLOTS + 1 + j]))
        start(stores[-2:])

    gather[0].finish()
    apply(0, order[2])
    gather[1].middle()
    for j in (order[3], order[0], order[1]):
        apply(0, j)
    gather[1].forward()
    for j in (order[2], order[3]):
        apply(1, j)
        put(j)
    gather[1].finish()
    for j in (order[0], order[1]):
        apply(1, j)
        put(j)
    for store in stores:
        store.wait()
    for k in range(PANELS):
        relay[k].drain()
        gather[k].drain()
    for each in whole:
        each.drain()
    scatter[1].drain()


def on_device(matrix):
    n = matrix.shape[0]
    scale = float(n * lax.axis_size("row")) ** 0.5
    dma = pltpu.SemaphoreType.DMA

    def vmem(*dims):
        return pltpu.VMEM(dims, F32)

    share = W // lax.axis_size("row")
    square = vmem(W, W)
    return pl.pallas_call(
        functools.partial(kernel, scale),
        out_shape=(
            jax.ShapeDtypeStruct((n, SLOTS, W), F32), jax.ShapeDtypeStruct((PANELS, share, SLOTS, W), F32),
        ),
        in_specs=[ANY],
        out_specs=(ANY, ANY),
        scratch_shapes=[
            vmem(SLOTS, n, W), vmem(n, W), vmem(n, W), vmem(n, W), vmem(n, W), vmem(n, W), square, square, square, square,
            square, vmem(8, LEAF), vmem(3, W, W), vmem(3, W, W), vmem(3, W // 2, W), vmem(3, 2, 3, 32, W), vmem(3, 2, 3, 8, W),
            vmem(SLOTS, W, W), vmem(2, 2, W, W), vmem(2, 2, 3, 128, W), vmem(2, 2, 3, 32, W), vmem(2, SLOTS, W, W),
            vmem(PANELS, SLOTS, share, W), vmem(2, 32, W), dma((192,)), dma((192,)), dma((16,)),
        ],
        compiler_params=pltpu.CompilerParams(
            collective_id=1, has_side_effects=True, vmem_limit_bytes=63 * 2**20
        ),
        name="qr",
    )(matrix)


def solution(mesh):
    return jax.shard_map(
        on_device,
        mesh=mesh,
        in_specs=(P("row", "col", None),),
        out_specs=(P("row", "col", None), P(None, "row", "col", None)),
        check_vma=False,
    )
```

```python
import functools

import jax
import jax.numpy as jnp
from jax import lax
from jax.experimental import pallas as pl
from jax.experimental.pallas import tpu as pltpu
from jax.sharding import PartitionSpec as P

PANELS = 2
W = 512
SLOTS = 4
NZ = 4
NY = 4
NX = 4
PIECES = 8
LEAF = 128
NEAR_FIRST = (0, 1, 3, 2)
HIGHEST = lax.Precision.HIGHEST
MESH = pl.DeviceIdType.MESH
F32 = jnp.float32
ANY = pl.BlockSpec(memory_space=pl.ANY)


def here():
    row = lax.axis_index("row")
    x = lax.axis_index("col")
    return x, lax.div(row, 2 * NZ), lax.rem(lax.div(row, 2), NZ), lax.rem(row, 2)


def device(dx=0, dy=0, dz=0, dc=0):
    x, y, z, c = here()
    x, y, z, c = lax.rem(x + dx, NX), lax.rem(y + dy, NY), lax.rem(z + dz, NZ), lax.rem(c + dc, 2)
    return ((y * NZ + z) * 2 + c, x)


def rows(start, size):
    return pl.ds(pl.multiple_of(start, 8), size)


def greet(peers):
    for peer in peers:
        pl.semaphore_signal(pltpu.get_barrier_semaphore(), inc=1, device_id=peer, device_id_type=MESH)


class Copies:
    def __init__(self, send, recv):
        self.send, self.recv, self.used = send, recv, 0

    def make(self, src, dst, peer):
        i = self.used
        self.used += 1
        return pltpu.make_async_remote_copy(
            src_ref=src, dst_ref=dst, send_sem=self.send.at[i], recv_sem=self.recv.at[i],
            device_id=peer, device_id_type=MESH,
        )


def start(copies):
    for copy in copies:
        copy.start()


def arrive(copies):
    for copy in copies:
        copy.wait_recv()


def drain(copies):
    for copy in copies:
        copy.wait_send()


def to_others(make, buf, at, size, into, axis, me, n):
    return [
        make(buf.at[rows(at + lax.rem(me + e, n) * size, size)], into.at[e - 1], device(**{axis: e})) for e in range(1, n)
    ]


def to_all(make, buf, at, size, axis, n):
    return [make(buf.at[rows(at, size)], buf.at[rows(at, size)], device(**{axis: e})) for e in range(1, n)]


class Reduce:
    def __init__(self, make, a_buf, a_at, b_buf, b_at, size, first, second):
        x, y, z, c = here()
        q = size // 4
        self.parts = []
        for i, (buf, at, one, two) in enumerate(((a_buf, a_at, ("dz", z), ("dy", y)), (b_buf, b_at, ("dy", y), ("dz", z)))):
            mid = at + one[1] * size
            end = mid + two[1] * q
            s1 = to_others(make, buf, at, size, first.at[i], one[0], one[1], 4)
            s2 = to_others(make, buf, mid, q, second.at[i], two[0], two[1], 4)
            self.parts.append((buf, mid, size, first.at[i], s1, end, q, second.at[i], s2))

    def begin(self):
        for p in self.parts:
            start(p[4])

    def middle(self):
        for buf, mid, size, into, s1, end, q, into2, s2 in self.parts:
            arrive(s1)
            buf[rows(mid, size)] = buf[rows(mid, size)] + ((into[0] + into[1]) + into[2])
            start(s2)

    def finish(self):
        for buf, mid, size, into, s1, end, q, into2, s2 in self.parts:
            arrive(s2)
            buf[rows(end, q)] = buf[rows(end, q)] + ((into2[0] + into2[1]) + into2[2])

    def drain(self):
        for p in self.parts:
            drain(p[4])
            drain(p[8])


class AllReduce:
    def __init__(self, make, g, out, g0, g1, g2):
        x, y, z, c = here()
        half = W // 2
        q = half // 2
        a0, b0 = c * half, c * half + q
        self.g, self.out, self.g0 = g, out, g0
        self.own = rows(c * half, half)
        self.core = make(g.at[rows((1 - c) * half, half)], g0, device(dc=1))
        self.red = Reduce(make, g, a0, g, b0, q // 4, g1, g2)
        self.ends = [(p[5], p[6]) for p in self.red.parts]
        self.s1 = to_all(make, out, self.ends[0][0], q // 16, "dy", NY) + to_all(make, out, self.ends[1][0], q // 16, "dz", NZ)
        self.s2 = to_all(make, out, a0 + z * (q // 4), q // 4, "dz", NZ) + to_all(make, out, b0 + y * (q // 4), q // 4, "dy", NY)
        self.last = make(out.at[self.own], out.at[self.own], device(dc=1))

    def keep(self):
        self.red.finish()
        for at, q in self.ends:
            self.out[rows(at, q)] = self.g[rows(at, q)]

    def drain_sums(self):
        self.red.drain()
        drain([self.core])

    def drain_shares(self):
        drain([self.last] + self.s1 + self.s2)

    def step(self, i):
        if i == 0:
            self.core.start()
        elif i == 1:
            self.core.wait_recv()
            self.g[self.own] = self.g[self.own] + self.g0[...]
            self.red.begin()
        elif i == 2:
            self.red.middle()
        elif i == 3:
            self.keep()
            start(self.s1)
        elif i == 4:
            arrive(self.s1)
            start(self.s2)
        elif i == 5:
            arrive(self.s2)
            self.last.start()
        else:
            self.last.wait_recv()

    def drain(self):
        self.drain_sums()
        self.drain_shares()


class Scatter:
    def __init__(self, make, h, h0, h1, h2):
        x, y, z, c = here()
        self.h, self.h0, self.c = h, h0, c
        self.core = [make(h.at[(1 - c) * 2 + i], h0.at[i], device(dc=1)) for i in range(2)]
        self.red = Reduce(make, h.at[c * 2], 0, h.at[c * 2 + 1], 0, W // 4, h1, h2)

    def add(self, i):
        self.core[i].wait_recv()
        self.h[self.c * 2 + i] = self.h[self.c * 2 + i] + self.h0[i]

    def part(self, i):
        p = self.red.parts[i]
        return p[0][rows(p[5], p[6])]

    def drain(self):
        self.red.drain()
        drain(self.core)


class Gather:
    def __init__(self, make, wt):
        x, y, z, c = here()
        self.wt = wt
        a, b = wt.at[c * 2], wt.at[c * 2 + 1]
        self.at = ((c * 2, z * 128 + y * 32), (c * 2 + 1, y * 128 + z * 32))
        self.s1 = to_all(make, a, z * 128 + y * 32, 32, "dy", NY) + to_all(make, b, y * 128 + z * 32, 32, "dz", NZ)
        self.s2a = to_all(make, a, z * 128, 128, "dz", NZ)
        self.s2b = to_all(make, b, y * 128, 128, "dy", NY)
        self.s3a = [self.pair(make, a, lax.rem(z + NZ - e, NZ) * 128) for e in range(NZ)]
        self.s3b = [self.pair(make, b, lax.rem(y + NY - e, NY) * 128) for e in range(NY)]

    def pair(self, make, buf, at):
        return make(buf.at[rows(at, 128)], buf.at[rows(at, 128)], device(dc=1))

    def begin(self):
        start(self.s1)

    def middle(self):
        arrive(self.s1)
        start([self.s3a[0], self.s3b[0]])
        for e in (1, 3):
            start([self.s2a[e - 1], self.s2b[e - 1]])

    def far(self):
        start([self.s2a[1], self.s2b[1]])

    def forward(self):
        for e in NEAR_FIRST[1:]:
            for i in range(2):
                self.take(e, i)

    def take(self, e, i):
        arrive([(self.s2a, self.s2b)[i][e - 1]])
        start([(self.s3a, self.s3b)[i][e]])

    def back(self, e, i):
        x, y, z, c = here()
        return lax.rem((z, y)[i] + NZ - e, NZ) * 128

    def finish(self):
        arrive(self.s3a)
        arrive(self.s3b)

    def drain(self):
        drain(self.s1 + self.s2a + self.s2b + self.s3a + self.s3b)


class Relay:
    def __init__(self, make, buf, root):
        x, y, z, c = here()
        half = W // 2
        step = half // PIECES
        self.d = lax.rem(x - root + NX, NX)
        self.right = [make(buf.at[pl.ds(i * step, step)], buf.at[pl.ds(i * step, step)], device(dx=1)) for i in range(PIECES)]
        self.left = [
            make(buf.at[pl.ds(half + i * step, step)], buf.at[pl.ds(half + i * step, step)], device(dx=NX - 1))
            for i in range(PIECES)
        ]

    def begin(self):
        @pl.when(self.d == 0)
        def _():
            for a, b in zip(self.right, self.left):
                a.start()
                b.start()

    def hop(self, i):
        a, b = self.right[i], self.left[i]

        @pl.when((self.d == 1) | (self.d == 2))
        def _():
            a.wait_recv()
            a.start()

        @pl.when((self.d == 2) | (self.d == 3))
        def _():
            b.wait_recv()
            b.start()

    def finish(self):
        @pl.when(self.d == 1)
        def _():
            arrive(self.left)

        @pl.when(self.d == 3)
        def _():
            arrive(self.right)

    def drain(self):
        @pl.when(self.d != 3)
        def _():
            drain(self.right)

        @pl.when(self.d != 1)
        def _():
            drain(self.left)


def split(value):
    high = value.astype(jnp.bfloat16)
    return high, (value - high.astype(F32)).astype(jnp.bfloat16)


def dot3(a, b, dims):
    dg = functools.partial(
        lax.dot_general, dimension_numbers=(dims, ((), ())), preferred_element_type=F32
    )
    return dg(a[0], b[0]) + (dg(a[0], b[1]) + dg(a[1], b[0]))


def dot6(a, b, dims):
    return lax.dot_general(a, b, (dims, ((), ())), precision=HIGHEST, preferred_element_type=F32)


OVER_ROWS = ((0,), (0,))
OVER_COLS = ((1,), (1,))
PLAIN = ((1,), (0,))


def lanes_of(v, k):
    return jnp.broadcast_to(v[:, k : k + 1], v.shape)


def sublanes_of(v, k):
    return jnp.broadcast_to(v[k : k + 1, :], v.shape)


def leaf_inverse(slabs, zero):
    n = len(slabs)
    lane = lax.broadcasted_iota(jnp.int32, zero.shape, 1)
    sub = lax.broadcasted_iota(jnp.int32, zero.shape, 0)
    slabs = list(slabs)
    for b in range(n):
        r = slabs[b]
        inside = (lane >= 8 * b) & (lane < 8 * b + 8)
        cols = [lanes_of(r, 8 * b + s) + zero for s in range(8)]
        d = [[sublanes_of(cols[s], t) for s in range(t + 1)] for t in range(8)]
        r = jnp.where(inside, jnp.where(lane == 8 * b + sub, 1.0, 0.0), r)
        line = [sublanes_of(r, s) for s in range(8)]
        ahead = b + 1 < n
        if ahead:
            e = [lanes_of(slabs[b + 1], 8 * b + s) for s in range(8)]
            nxt = jnp.where(inside, 0.0, slabs[b + 1])
        rp = [None] * 8
        m = {}
        for s in range(8):
            rp[s] = 1.0 / d[s][s]
            if ahead:
                f = e[s] * rp[s]
                nxt = nxt - f * line[s]
                for u in range(s + 1, 8):
                    e[u] = e[u] - f * d[u][s]
            for t in range(s + 1, 8):
                m[t, s] = d[t][s] * rp[s]
            for t in range(s + 1, 8):
                for u in range(s + 1, t + 1):
                    d[t][u] = d[t][u] - m[t, s] * d[u][s]
                line[t] = line[t] - m[t, s] * line[s]
        out, pivot = line[0], d[0][0]
        for s in range(1, 8):
            out = jnp.where(sub == s, line[s], out)
            pivot = jnp.where(sub == s, d[s][s], pivot)
        slabs[b] = out * (1.0 / jnp.sqrt(pivot))
        if ahead:
            slabs[b + 1] = nxt
        if b + 2 < n:
            z = [None] * 8
            for s in reversed(range(8)):
                z[s] = line[s] * rp[s]
                for t in range(s + 1, 8):
                    z[s] = z[s] - m[t, s] * z[t]
            for i in range(b + 2, n):
                acc = jnp.where(inside, 0.0, slabs[i])
                for s in range(8):
                    acc = acc - lanes_of(slabs[i], 8 * b + s) * z[s]
                slabs[i] = acc
    return slabs


def factor(z_ref, u_ref, zero_ref, middle, end):
    w = LEAF
    ri = lax.broadcasted_iota(jnp.int32, (w, w), 0)
    ci = lax.broadcasted_iota(jnp.int32, (w, w), 1)
    wide = lax.broadcasted_iota(jnp.int32, (w, W), 1)
    down = lax.broadcasted_iota(jnp.int32, (w, W), 0)

    @pl.loop(0, W // w)
    def _(j):
        here = pl.ds(pl.multiple_of(j * w, w), w)
        block = z_ref[here, here]
        y = jnp.concatenate(leaf_inverse([block[8 * i : 8 * i + 8] for i in range(w // 8)], zero_ref[...]), axis=0)
        y = jnp.where(ci <= ri, y, 0.0)
        t = dot6(y, z_ref[here, :], PLAIN)
        u_ref[here, :] = jnp.where(wide >= j * w + down, t, 0.0)
        z_ref[here, :] = t
        z_ref[here, here] = y
        for step, do in middle.items():
            pl.when(j == step)(do)

        @pl.loop(j + 1, W // w)
        def _(i):
            there = pl.ds(pl.multiple_of(i * w, w), w)
            z_ref[there, here] = jnp.zeros((w, w), F32)
            z_ref[there, :] = z_ref[there, :] - dot6(u_ref[here, there], z_ref[here, :], OVER_ROWS)

        for step, do in end.items():
            pl.when(j == step)(do)

    @pl.loop(0, W // w)
    def _(j):
        here = pl.ds(pl.multiple_of(j * w, w), w)
        z_ref[here, :] = jnp.where(wide <= j * w + down, z_ref[here, :], 0.0)


def kernel(scale, x_ref, x_out, r_out, xs, p0, p1, pn, q0, q1, w01, z0, z1, u0, u1, zero, g, gf, g0, g1, g2,
           h, h0, h1, h2, wt, up, fix, ha, hb, send, recv, local):
    x, y, z, c = here()
    make = Copies(send, recv).make
    other = 1 - c
    loads = [pltpu.make_async_copy(x_ref.at[:, j, :], xs.at[j], local.at[j]) for j in range(SLOTS)]
    seeds = [pltpu.make_async_copy(x_ref.at[:, 0, :], p, local.at[SLOTS]) for p in (p0, p1)]
    for k in range(PANELS):
        @pl.when(x == k)
        def _():
            seeds[k].start()
    start(loads)
    zero[...] = jnp.zeros_like(zero)
    relay = [Relay(make, p, k) for k, p in enumerate((p0, p1))]
    whole = [AllReduce(make, g.at[i], gf.at[i], g0.at[i], g1.at[i], g2.at[i]) for i in range(3)]
    scatter = [Scatter(make, h, h0.at[k], h1.at[k], h2.at[k]) for k in range(PANELS)]
    gather = [Gather(make, wt.at[k]) for k in range(PANELS)]
    peers = [device(dc=1)] + [device(dz=d) for d in range(1, NZ)] + [device(dy=d) for d in range(1, NY)]
    peers += [device(dx=d) for d in range(1, NX)]
    greet(peers)

    @pl.when(x == 0)
    def _():
        seeds[0].wait()
        g[0] = dot6(p0[...], p0[...], OVER_ROWS)

    @pl.when(x == 1)
    def _():
        seeds[1].wait()

    pl.semaphore_wait(pltpu.get_barrier_semaphore(), len(peers))
    relay[0].begin()
    across = [
        [make(gf.at[0, rows(at, q)], gf.at[0, rows(at, q)], device(dx=e)) for at, q in whole[0].ends] for e in range(1, NX)
    ]

    @pl.when(x == 0)
    def _():
        for i in range(3):
            whole[0].step(i)
        whole[0].keep()
        for copies in across:
            start(copies)

    for i in range(PIECES):
        relay[0].hop(i)
    relay[1].begin()
    for e in range(1, NX):
        @pl.when(x == e)
        def _():
            arrive(across[e - 1])

    start(whole[0].s1)

    @pl.when(x != 3)
    def _():
        for i in range(2):
            relay[1].hop(i)

    relay[0].finish()
    for load in loads:
        load.wait()

    def hops(*pieces):
        for i in pieces:
            relay[1].hop(i)

    def terms(panel, steps):
        ha[0], ha[1] = split(panel[...])

        @pl.loop(0, SLOTS)
        def _(i):
            j = lax.rem(other * 2 + i, SLOTS)
            h[j] = dot3(split(xs[j]), (ha[0], ha[1]), OVER_ROWS)
            for step, do in enumerate(steps):
                pl.when(i == step)(do)

    def zero_first():
        scatter[0].core[0].start()
        whole[0].step(4)

        @pl.when(x == 3)
        def _():
            hops(0, 1)

        hops(2, 3)

    def zero_second():
        scatter[0].core[1].start()
        hops(4)
        whole[0].step(5)
        hops(5)

    terms(p0, (zero_first, zero_second, lambda: hops(6), lambda: hops(7)))
    for i in range(2):
        scatter[0].add(i)
    scatter[0].red.begin()
    whole[0].step(6)
    z0[...] = gf[0]

    def cross():
        relay[1].finish()
        g[1] = dot6(p0[...], p1[...], OVER_ROWS)
        whole[1].step(0)

    factor(
        z0, u0, zero, {0: cross, 2: lambda: whole[1].step(3), 3: lambda: whole[1].step(4)},
        {0: lambda: whole[1].step(1), 1: lambda: whole[1].step(2), 2: scatter[0].red.middle},
    )
    scatter[0].red.finish()
    inverse = z0[...]

    def shards(k, parts, inv):
        both = dot6(jnp.concatenate(parts, axis=0), inv, OVER_COLS)
        for i, (slot, at) in enumerate(gather[k].at):
            wt[k, slot, rows(at, 32)] = both[32 * i : 32 * i + 32]

    shards(0, [scatter[0].part(i) for i in range(2)], inverse)
    gather[0].begin()
    q0[...] = dot6(p0[...], inverse, OVER_COLS)
    hb[0], hb[1] = split(q0[...])
    whole[1].step(5)
    whole[1].step(6)
    w01[...] = dot6(inverse, gf[1], PLAIN)
    gather[0].middle()
    gather[0].far()

    pn[...] = p1[...] - dot6(q0[...], w01[...], PLAIN)
    g[2] = dot6(pn[...], pn[...], OVER_ROWS)
    whole[2].step(0)

    row = (y * NZ + z) * 2 + c
    mine = rows(row * 16, 16)
    pick = jnp.where(
        lax.broadcasted_iota(jnp.int32, (16, W), 1) == row * 16 + lax.broadcasted_iota(jnp.int32, (16, W), 0), 1.0, 0.0
    ).astype(F32)

    scatter[0].drain()

    def one_first():
        scatter[1].core[0].start()
        whole[2].step(1)

    terms(p1, (one_first, scatter[1].core[1].start, lambda: whole[2].step(2), lambda: whole[2].step(3)))
    gather[0].forward()
    for i in range(2):
        scatter[1].add(i)
    both = dot6(jnp.concatenate([wt[0, slot, rows(at, 32)] for slot, at in gather[0].at], axis=0), w01[...], PLAIN)
    for i in range(2):
        fix[i] = both[32 * i : 32 * i + 32]
    whole[2].step(4)
    whole[2].step(5)
    scatter[1].red.begin()
    whole[2].step(6)
    z1[...] = gf[2]
    factor(z1, u1, zero, {2: scatter[1].red.middle}, {})
    scatter[1].red.finish()
    inverse = z1[...]
    shards(1, [scatter[1].part(i) - fix[i] for i in range(2)], inverse)
    gather[1].begin()
    q1[...] = dot6(pn[...], inverse, OVER_COLS)
    ha[0], ha[1] = split(q1[...])
    gather[0].finish()
    gather[1].middle()
    gather[1].far()

    @pl.loop(0, SLOTS)
    def _(j):
        w = wt[0, j]
        new = xs[j] - dot3((hb[0], hb[1]), split(w), OVER_COLS)
        owner = (j == 0) & (x == 0)
        xs[j] = jnp.where(owner, q0[...] * scale, new)
        up[0, j] = jnp.where(owner, u0[mine], dot6(pick, w, OVER_COLS))

    def blocks(n):
        turn = lax.div(n, 2)
        e = turn + jnp.where(turn == 2, 1, 0) - jnp.where(turn == 3, 1, 0)
        slot = lax.rem(c + lax.rem(n, 2), 2) * 2
        return [(slot + i, pl.ds(pl.multiple_of(gather[1].back(e, i), 128), 128)) for i in range(2)]

    def ready(n):
        e = NEAR_FIRST[n // 2]
        if n % 2:
            arrive([gather[1].s3a[e], gather[1].s3b[e]])
        elif e:
            gather[1].take(e, 0)
            gather[1].take(e, 1)

    def store(n, i, j, lanes):
        return pltpu.make_async_copy(xs.at[j, :, lanes], x_out.at[:, j, lanes], local.at[SLOTS + 1 + 2 * n + i])

    @pl.loop(0, 2 * NZ)
    def _(n):
        for step in range(2 * NZ):
            pl.when(n == step)(functools.partial(ready, step))
        pair = blocks(n)
        w = jnp.concatenate([wt[1, j, lanes] for j, lanes in pair], axis=0)
        product = dot3((ha[0], ha[1]), split(w), OVER_COLS)
        line = dot6(pick, w, OVER_COLS)
        for i, (j, lanes) in enumerate(pair):
            own = slice(128 * i, 128 * i + 128)
            old = xs[j, :, lanes]
            skip = (j == 0) & (x < 1)
            owner = (j == 0) & (x == 1)
            xs[j, :, lanes] = jnp.where(skip, old, jnp.where(owner, q1[:, lanes] * scale, old - product[:, own]))
            up[1, j, :, lanes] = jnp.where(skip, 0.0, jnp.where(owner, u1[mine, lanes], line[:, own]))
            store(n, i, j, lanes).start()

    stores = []

    def keep(source, target):
        stores.append(pltpu.make_async_copy(source, target, local.at[SLOTS + 1 + 4 * NZ + len(stores)]))
        stores[-1].start()

    for k in range(PANELS):
        for j in range(SLOTS):
            keep(up.at[k, j], r_out.at[k, :, j, :])
    for each in stores:
        each.wait()

    @pl.loop(0, 2 * NZ)
    def _(n):
        for i, (j, lanes) in enumerate(blocks(n)):
            store(n, i, j, lanes).wait()

    for k in range(PANELS):
        relay[k].drain()
        gather[k].drain()

    @pl.when(x == 0)
    def _():
        whole[0].drain_sums()
        for copies in across:
            drain(copies)

    whole[0].drain_shares()
    whole[1].drain()
    whole[2].drain()
    scatter[1].drain()


def on_device(matrix):
    n = matrix.shape[0]
    scale = float(n * lax.axis_size("row")) ** 0.5
    dma = pltpu.SemaphoreType.DMA

    def vmem(*dims):
        return pltpu.VMEM(dims, F32)

    share = W // lax.axis_size("row")
    square = vmem(W, W)
    return pl.pallas_call(
        functools.partial(kernel, scale),
        out_shape=(
            jax.ShapeDtypeStruct((n, SLOTS, W), F32), jax.ShapeDtypeStruct((PANELS, share, SLOTS, W), F32),
        ),
        in_specs=[ANY],
        out_specs=(ANY, ANY),
        scratch_shapes=[
            vmem(SLOTS, n, W), vmem(n, W), vmem(n, W), vmem(n, W), vmem(n, W), vmem(n, W), square, square, square, square,
            square, vmem(8, LEAF), vmem(3, W, W), vmem(3, W, W), vmem(3, W // 2, W), vmem(3, 2, 3, 32, W), vmem(3, 2, 3, 8, W),
            vmem(SLOTS, W, W), vmem(2, 2, W, W), vmem(2, 2, 3, 128, W), vmem(2, 2, 3, 32, W), vmem(2, SLOTS, W, W),
            vmem(PANELS, SLOTS, share, W), vmem(2, 32, W), pltpu.VMEM((2, W, W), jnp.bfloat16),
            pltpu.VMEM((2, W, W), jnp.bfloat16), dma((208,)), dma((208,)), dma((32,)),
        ],
        compiler_params=pltpu.CompilerParams(
            collective_id=1, has_side_effects=True, vmem_limit_bytes=63 * 2**20
        ),
        name="qr",
    )(matrix)


def solution(mesh):
    return jax.shard_map(
        on_device,
        mesh=mesh,
        in_specs=(P("row", "col", None),),
        out_specs=(P("row", "col", None), P(None, "row", "col", None)),
        check_vma=False,
    )
```

```python
import functools

import jax
import jax.numpy as jnp
from jax import lax
from jax.experimental import pallas as pl
from jax.experimental.pallas import tpu as pltpu
from jax.sharding import PartitionSpec as P

PANELS = 2
W = 512
SLOTS = 4
NZ = 4
NY = 4
NX = 4
PIECES = 8
LEAF = 128
NEAR_FIRST = (0, 1, 3, 2)
HIGHEST = lax.Precision.HIGHEST
MESH = pl.DeviceIdType.MESH
F32 = jnp.float32
ANY = pl.BlockSpec(memory_space=pl.ANY)


def here():
    row = lax.axis_index("row")
    x = lax.axis_index("col")
    return x, lax.div(row, 2 * NZ), lax.rem(lax.div(row, 2), NZ), lax.rem(row, 2)


def device(dx=0, dy=0, dz=0, dc=0):
    x, y, z, c = here()
    x, y, z, c = lax.rem(x + dx, NX), lax.rem(y + dy, NY), lax.rem(z + dz, NZ), lax.rem(c + dc, 2)
    return ((y * NZ + z) * 2 + c, x)


def rows(start, size):
    return pl.ds(pl.multiple_of(start, 8), size)


def greet(peers):
    for peer in peers:
        pl.semaphore_signal(pltpu.get_barrier_semaphore(), inc=1, device_id=peer, device_id_type=MESH)


class Copies:
    def __init__(self, send, recv):
        self.send, self.recv, self.used = send, recv, 0

    def make(self, src, dst, peer):
        i = self.used
        self.used += 1
        return pltpu.make_async_remote_copy(
            src_ref=src, dst_ref=dst, send_sem=self.send.at[i], recv_sem=self.recv.at[i],
            device_id=peer, device_id_type=MESH,
        )


def start(copies):
    for copy in copies:
        copy.start()


def arrive(copies):
    for copy in copies:
        copy.wait_recv()


def drain(copies):
    for copy in copies:
        copy.wait_send()


def to_others(make, buf, at, size, into, axis, me, n):
    return [
        make(buf.at[rows(at + lax.rem(me + e, n) * size, size)], into.at[e - 1], device(**{axis: e})) for e in range(1, n)
    ]


def to_all(make, buf, at, size, axis, n):
    return [make(buf.at[rows(at, size)], buf.at[rows(at, size)], device(**{axis: e})) for e in range(1, n)]


class Reduce:
    def __init__(self, make, a_buf, a_at, b_buf, b_at, size, first, second):
        x, y, z, c = here()
        q = size // 4
        self.parts = []
        for i, (buf, at, one, two) in enumerate(((a_buf, a_at, ("dz", z), ("dy", y)), (b_buf, b_at, ("dy", y), ("dz", z)))):
            mid = at + one[1] * size
            end = mid + two[1] * q
            s1 = to_others(make, buf, at, size, first.at[i], one[0], one[1], 4)
            s2 = to_others(make, buf, mid, q, second.at[i], two[0], two[1], 4)
            self.parts.append((buf, mid, size, first.at[i], s1, end, q, second.at[i], s2))

    def begin(self):
        for p in self.parts:
            start(p[4])

    def middle(self):
        for buf, mid, size, into, s1, end, q, into2, s2 in self.parts:
            arrive(s1)
            buf[rows(mid, size)] = buf[rows(mid, size)] + ((into[0] + into[1]) + into[2])
            start(s2)

    def finish(self):
        for buf, mid, size, into, s1, end, q, into2, s2 in self.parts:
            arrive(s2)
            buf[rows(end, q)] = buf[rows(end, q)] + ((into2[0] + into2[1]) + into2[2])

    def drain(self):
        for p in self.parts:
            drain(p[4])
            drain(p[8])


class AllReduce:
    def __init__(self, make, g, out, g0, g1, g2):
        x, y, z, c = here()
        half = W // 2
        q = half // 2
        a0, b0 = c * half, c * half + q
        self.g, self.out, self.g0 = g, out, g0
        self.own = rows(c * half, half)
        self.core = make(g.at[rows((1 - c) * half, half)], g0, device(dc=1))
        self.red = Reduce(make, g, a0, g, b0, q // 4, g1, g2)
        self.ends = [(p[5], p[6]) for p in self.red.parts]
        self.s1 = to_all(make, out, self.ends[0][0], q // 16, "dy", NY) + to_all(make, out, self.ends[1][0], q // 16, "dz", NZ)
        self.s2 = to_all(make, out, a0 + z * (q // 4), q // 4, "dz", NZ) + to_all(make, out, b0 + y * (q // 4), q // 4, "dy", NY)
        self.last = make(out.at[self.own], out.at[self.own], device(dc=1))

    def keep(self):
        self.red.finish()
        for at, q in self.ends:
            self.out[rows(at, q)] = self.g[rows(at, q)]

    def drain_sums(self):
        self.red.drain()
        drain([self.core])

    def drain_shares(self):
        drain([self.last] + self.s1 + self.s2)

    def step(self, i):
        if i == 0:
            self.core.start()
        elif i == 1:
            self.core.wait_recv()
            self.g[self.own] = self.g[self.own] + self.g0[...]
            self.red.begin()
        elif i == 2:
            self.red.middle()
        elif i == 3:
            self.keep()
            start(self.s1)
        elif i == 4:
            arrive(self.s1)
            start(self.s2)
        elif i == 5:
            arrive(self.s2)
            self.last.start()
        else:
            self.last.wait_recv()

    def drain(self):
        self.drain_sums()
        self.drain_shares()


class Scatter:
    def __init__(self, make, h, h0, h1, h2):
        x, y, z, c = here()
        self.h, self.h0, self.c = h, h0, c
        self.core = [make(h.at[(1 - c) * 2 + i], h0.at[i], device(dc=1)) for i in range(2)]
        self.red = Reduce(make, h.at[c * 2], 0, h.at[c * 2 + 1], 0, W // 4, h1, h2)

    def add(self, i):
        self.core[i].wait_recv()
        self.h[self.c * 2 + i] = self.h[self.c * 2 + i] + self.h0[i]

    def part(self, i):
        p = self.red.parts[i]
        return p[0][rows(p[5], p[6])]

    def drain(self):
        self.red.drain()
        drain(self.core)


class Gather:
    def __init__(self, make, wt):
        x, y, z, c = here()
        self.wt = wt
        a, b = wt.at[c * 2], wt.at[c * 2 + 1]
        self.at = ((c * 2, z * 128 + y * 32), (c * 2 + 1, y * 128 + z * 32))
        self.s1 = to_all(make, a, z * 128 + y * 32, 32, "dy", NY) + to_all(make, b, y * 128 + z * 32, 32, "dz", NZ)
        self.s2a = to_all(make, a, z * 128, 128, "dz", NZ)
        self.s2b = to_all(make, b, y * 128, 128, "dy", NY)
        self.s3a = [self.pair(make, a, lax.rem(z + NZ - e, NZ) * 128) for e in range(NZ)]
        self.s3b = [self.pair(make, b, lax.rem(y + NY - e, NY) * 128) for e in range(NY)]

    def pair(self, make, buf, at):
        return make(buf.at[rows(at, 128)], buf.at[rows(at, 128)], device(dc=1))

    def begin(self):
        start(self.s1)

    def middle(self):
        arrive(self.s1)
        start([self.s3a[0], self.s3b[0]])
        for e in (1, 3):
            start([self.s2a[e - 1], self.s2b[e - 1]])

    def far(self):
        start([self.s2a[1], self.s2b[1]])

    def forward(self):
        for e in NEAR_FIRST[1:]:
            for i in range(2):
                self.take(e, i)

    def take(self, e, i):
        arrive([(self.s2a, self.s2b)[i][e - 1]])
        start([(self.s3a, self.s3b)[i][e]])

    def back(self, e, i):
        x, y, z, c = here()
        return lax.rem((z, y)[i] + NZ - e, NZ) * 128

    def finish(self):
        arrive(self.s3a)
        arrive(self.s3b)

    def drain(self):
        drain(self.s1 + self.s2a + self.s2b + self.s3a + self.s3b)


class Relay:
    def __init__(self, make, buf, root):
        x, y, z, c = here()
        half = W // 2
        step = half // PIECES
        self.d = lax.rem(x - root + NX, NX)
        self.right = [make(buf.at[pl.ds(i * step, step)], buf.at[pl.ds(i * step, step)], device(dx=1)) for i in range(PIECES)]
        self.left = [
            make(buf.at[pl.ds(half + i * step, step)], buf.at[pl.ds(half + i * step, step)], device(dx=NX - 1))
            for i in range(PIECES)
        ]

    def begin(self):
        @pl.when(self.d == 0)
        def _():
            for a, b in zip(self.right, self.left):
                a.start()
                b.start()

    def hop(self, i):
        a, b = self.right[i], self.left[i]

        @pl.when((self.d == 1) | (self.d == 2))
        def _():
            a.wait_recv()
            a.start()

        @pl.when((self.d == 2) | (self.d == 3))
        def _():
            b.wait_recv()
            b.start()

    def finish(self):
        @pl.when(self.d == 1)
        def _():
            arrive(self.left)

        @pl.when(self.d == 3)
        def _():
            arrive(self.right)

    def drain(self):
        @pl.when(self.d != 3)
        def _():
            drain(self.right)

        @pl.when(self.d != 1)
        def _():
            drain(self.left)


def split(value):
    high = value.astype(jnp.bfloat16)
    return high, (value - high.astype(F32)).astype(jnp.bfloat16)


def dot3(a, b, dims):
    dg = functools.partial(
        lax.dot_general, dimension_numbers=(dims, ((), ())), preferred_element_type=F32
    )
    return dg(a[0], b[0]) + (dg(a[0], b[1]) + dg(a[1], b[0]))


def dot6(a, b, dims):
    return lax.dot_general(a, b, (dims, ((), ())), precision=HIGHEST, preferred_element_type=F32)


OVER_ROWS = ((0,), (0,))
OVER_COLS = ((1,), (1,))
PLAIN = ((1,), (0,))


def lanes_of(v, k):
    return jnp.broadcast_to(v[:, k : k + 1], v.shape)


def sublanes_of(v, k):
    return jnp.broadcast_to(v[k : k + 1, :], v.shape)


def leaf_inverse(slabs, zero):
    n = len(slabs)
    lane = lax.broadcasted_iota(jnp.int32, zero.shape, 1)
    sub = lax.broadcasted_iota(jnp.int32, zero.shape, 0)
    slabs = list(slabs)
    for b in range(n):
        r = slabs[b]
        inside = (lane >= 8 * b) & (lane < 8 * b + 8)
        cols = [lanes_of(r, 8 * b + s) + zero for s in range(8)]
        d = [[sublanes_of(cols[s], t) for s in range(t + 1)] for t in range(8)]
        r = jnp.where(inside, jnp.where(lane == 8 * b + sub, 1.0, 0.0), r)
        line = [sublanes_of(r, s) for s in range(8)]
        ahead = b + 1 < n
        if ahead:
            e = [lanes_of(slabs[b + 1], 8 * b + s) for s in range(8)]
            nxt = jnp.where(inside, 0.0, slabs[b + 1])
        rp = [None] * 8
        m = {}
        for s in range(8):
            rp[s] = 1.0 / d[s][s]
            if ahead:
                f = e[s] * rp[s]
                nxt = nxt - f * line[s]
                for u in range(s + 1, 8):
                    e[u] = e[u] - f * d[u][s]
            for t in range(s + 1, 8):
                m[t, s] = d[t][s] * rp[s]
            for t in range(s + 1, 8):
                for u in range(s + 1, t + 1):
                    d[t][u] = d[t][u] - m[t, s] * d[u][s]
                line[t] = line[t] - m[t, s] * line[s]
        out, pivot = line[0], d[0][0]
        for s in range(1, 8):
            out = jnp.where(sub == s, line[s], out)
            pivot = jnp.where(sub == s, d[s][s], pivot)
        slabs[b] = out * (1.0 / jnp.sqrt(pivot))
        if ahead:
            slabs[b + 1] = nxt
        if b + 2 < n:
            z = [None] * 8
            for s in reversed(range(8)):
                z[s] = line[s] * rp[s]
                for t in range(s + 1, 8):
                    z[s] = z[s] - m[t, s] * z[t]
            for i in range(b + 2, n):
                acc = jnp.where(inside, 0.0, slabs[i])
                for s in range(8):
                    acc = acc - lanes_of(slabs[i], 8 * b + s) * z[s]
                slabs[i] = acc
    return slabs


def factor(z_ref, u_ref, zero_ref, middle, end):
    w = LEAF
    ri = lax.broadcasted_iota(jnp.int32, (w, w), 0)
    ci = lax.broadcasted_iota(jnp.int32, (w, w), 1)
    wide = lax.broadcasted_iota(jnp.int32, (w, W), 1)
    down = lax.broadcasted_iota(jnp.int32, (w, W), 0)

    @pl.loop(0, W // w)
    def _(j):
        here = pl.ds(pl.multiple_of(j * w, w), w)
        block = z_ref[here, here]
        y = jnp.concatenate(leaf_inverse([block[8 * i : 8 * i + 8] for i in range(w // 8)], zero_ref[...]), axis=0)
        y = jnp.where(ci <= ri, y, 0.0)
        t = dot6(y, z_ref[here, :], PLAIN)
        u_ref[here, :] = jnp.where(wide >= j * w + down, t, 0.0)
        z_ref[here, :] = t
        z_ref[here, here] = y
        for step, do in middle.items():
            pl.when(j == step)(do)

        @pl.loop(j + 1, W // w)
        def _(i):
            there = pl.ds(pl.multiple_of(i * w, w), w)
            z_ref[there, here] = jnp.zeros((w, w), F32)
            z_ref[there, :] = z_ref[there, :] - dot6(u_ref[here, there], z_ref[here, :], OVER_ROWS)

        for step, do in end.items():
            pl.when(j == step)(do)

    @pl.loop(0, W // w)
    def _(j):
        here = pl.ds(pl.multiple_of(j * w, w), w)
        z_ref[here, :] = jnp.where(wide <= j * w + down, z_ref[here, :], 0.0)


def kernel(scale, x_ref, x_out, r_out, xs, p0, p1, pn, q0, q1, w01, z0, z1, u0, u1, zero, g, gf, g0, g1, g2,
           h, h0, h1, h2, wt, up, fix, ha, hb, send, recv, local):
    x, y, z, c = here()
    make = Copies(send, recv).make
    other = 1 - c
    loads = [pltpu.make_async_copy(x_ref.at[:, j, :], xs.at[j], local.at[j]) for j in range(SLOTS)]
    seeds = [pltpu.make_async_copy(x_ref.at[:, 0, :], p, local.at[SLOTS]) for p in (p0, p1)]
    for k in range(PANELS):
        @pl.when(x == k)
        def _():
            seeds[k].start()
    start(loads)
    zero[...] = jnp.zeros_like(zero)
    relay = [Relay(make, p, k) for k, p in enumerate((p0, p1))]
    whole = [AllReduce(make, g.at[i], gf.at[i], g0.at[i], g1.at[i], g2.at[i]) for i in range(3)]
    scatter = [Scatter(make, h, h0.at[k], h1.at[k], h2.at[k]) for k in range(PANELS)]
    gather = [Gather(make, wt.at[k]) for k in range(PANELS)]
    peers = [device(dc=1)] + [device(dz=d) for d in range(1, NZ)] + [device(dy=d) for d in range(1, NY)]
    peers += [device(dx=d) for d in range(1, NX)]
    greet(peers)

    @pl.when(x == 0)
    def _():
        seeds[0].wait()
        g[0] = dot6(p0[...], p0[...], OVER_ROWS)

    @pl.when(x == 1)
    def _():
        seeds[1].wait()

    pl.semaphore_wait(pltpu.get_barrier_semaphore(), len(peers))
    relay[0].begin()
    across = [
        [make(gf.at[0, rows(at, q)], gf.at[0, rows(at, q)], device(dx=e)) for at, q in whole[0].ends] for e in range(1, NX)
    ]

    @pl.when(x == 0)
    def _():
        for i in range(3):
            whole[0].step(i)
        whole[0].keep()
        for copies in across:
            start(copies)

    for i in range(PIECES):
        relay[0].hop(i)
    relay[1].begin()
    for e in range(1, NX):
        @pl.when(x == e)
        def _():
            arrive(across[e - 1])

    start(whole[0].s1)

    @pl.when(x != 3)
    def _():
        for i in range(2):
            relay[1].hop(i)

    relay[0].finish()
    for load in loads:
        load.wait()

    def hops(*pieces):
        for i in pieces:
            relay[1].hop(i)

    def terms(panel, steps):
        ha[0, :W], ha[1, :W] = split(panel[...])

        @pl.loop(0, SLOTS)
        def _(i):
            j = lax.rem(other * 2 + i, SLOTS)
            h[j] = dot3(split(xs[j]), (ha[0, :W], ha[1, :W]), OVER_ROWS)
            for step, do in enumerate(steps):
                pl.when(i == step)(do)

    def zero_first():
        scatter[0].core[0].start()
        whole[0].step(4)

        @pl.when(x == 3)
        def _():
            hops(0, 1)

        hops(2, 3)

    def zero_second():
        scatter[0].core[1].start()
        hops(4)
        whole[0].step(5)
        hops(5)

    terms(p0, (zero_first, zero_second, lambda: hops(6), lambda: hops(7)))
    for i in range(2):
        scatter[0].add(i)
    scatter[0].red.begin()
    whole[0].step(6)
    z0[...] = gf[0]

    def cross():
        relay[1].finish()
        g[1] = dot6(p0[...], p1[...], OVER_ROWS)
        whole[1].step(0)

    factor(
        z0, u0, zero, {0: cross, 2: lambda: whole[1].step(3), 3: lambda: whole[1].step(4)},
        {0: lambda: whole[1].step(1), 1: lambda: whole[1].step(2), 2: scatter[0].red.middle},
    )
    scatter[0].red.finish()
    inverse = z0[...]

    def shards(k, parts, inv):
        both = dot6(jnp.concatenate(parts, axis=0), inv, OVER_COLS)
        for i, (slot, at) in enumerate(gather[k].at):
            wt[k, slot, rows(at, 32)] = both[32 * i : 32 * i + 32]

    shards(0, [scatter[0].part(i) for i in range(2)], inverse)
    gather[0].begin()
    q0[...] = dot6(p0[...], inverse, OVER_COLS)
    hb[0, :W], hb[1, :W] = split(q0[...])
    whole[1].step(5)
    whole[1].step(6)
    w01[...] = dot6(inverse, gf[1], PLAIN)
    gather[0].middle()
    gather[0].far()

    pn[...] = p1[...] - dot6(q0[...], w01[...], PLAIN)
    g[2] = dot6(pn[...], pn[...], OVER_ROWS)
    whole[2].step(0)

    row = (y * NZ + z) * 2 + c
    mine = rows(row * 16, 16)
    pick = jnp.where(
        lax.broadcasted_iota(jnp.int32, (16, W), 1) == row * 16 + lax.broadcasted_iota(jnp.int32, (16, W), 0), 1.0, 0.0
    )
    for each in (ha, hb):
        each[0, W:] = pick.astype(jnp.bfloat16)
        each[1, W:] = jnp.zeros(pick.shape, jnp.bfloat16)

    scatter[0].drain()

    def one_first():
        scatter[1].core[0].start()
        whole[2].step(1)

    terms(p1, (one_first, scatter[1].core[1].start, lambda: whole[2].step(2), lambda: whole[2].step(3)))
    gather[0].forward()
    for i in range(2):
        scatter[1].add(i)
    both = dot6(jnp.concatenate([wt[0, slot, rows(at, 32)] for slot, at in gather[0].at], axis=0), w01[...], PLAIN)
    for i in range(2):
        fix[i] = both[32 * i : 32 * i + 32]
    whole[2].step(4)
    whole[2].step(5)
    scatter[1].red.begin()
    whole[2].step(6)
    z1[...] = gf[2]
    factor(z1, u1, zero, {2: scatter[1].red.middle}, {})
    scatter[1].red.finish()
    inverse = z1[...]
    shards(1, [scatter[1].part(i) - fix[i] for i in range(2)], inverse)
    gather[1].begin()
    q1[...] = dot6(pn[...], inverse, OVER_COLS)
    ha[0, :W], ha[1, :W] = split(q1[...])
    gather[0].finish()
    gather[1].middle()
    gather[1].far()

    @pl.loop(0, SLOTS)
    def _(j):
        w = wt[0, j]
        product = dot3((hb[0], hb[1]), split(w), OVER_COLS)
        owner = (j == 0) & (x == 0)
        xs[j] = jnp.where(owner, q0[...] * scale, xs[j] - product[:W])
        up[0, j] = jnp.where(owner, u0[mine], product[W:])

    def blocks(n):
        turn = lax.div(n, 2)
        e = turn + jnp.where(turn == 2, 1, 0) - jnp.where(turn == 3, 1, 0)
        slot = lax.rem(c + lax.rem(n, 2), 2) * 2
        return [(slot + i, pl.ds(pl.multiple_of(gather[1].back(e, i), 128), 128)) for i in range(2)]

    def ready(n):
        e = NEAR_FIRST[n // 2]
        if n % 2:
            arrive([gather[1].s3a[e], gather[1].s3b[e]])
        elif e:
            gather[1].take(e, 0)
            gather[1].take(e, 1)

    def store(n, i, j, lanes):
        return pltpu.make_async_copy(xs.at[j, :, lanes], x_out.at[:, j, lanes], local.at[SLOTS + 1 + 2 * n + i])

    @pl.loop(0, 2 * NZ)
    def _(n):
        for step in range(2 * NZ):
            pl.when(n == step)(functools.partial(ready, step))
        pair = blocks(n)
        w = jnp.concatenate([wt[1, j, lanes] for j, lanes in pair], axis=0)
        product = dot3((ha[0], ha[1]), split(w), OVER_COLS)
        for i, (j, lanes) in enumerate(pair):
            own = slice(128 * i, 128 * i + 128)
            old = xs[j, :, lanes]
            skip = (j == 0) & (x < 1)
            owner = (j == 0) & (x == 1)
            xs[j, :, lanes] = jnp.where(skip, old, jnp.where(owner, q1[:, lanes] * scale, old - product[:W, own]))
            up[1, j, :, lanes] = jnp.where(skip, 0.0, jnp.where(owner, u1[mine, lanes], product[W:, own]))
            store(n, i, j, lanes).start()

    stores = []

    def keep(source, target):
        stores.append(pltpu.make_async_copy(source, target, local.at[SLOTS + 1 + 4 * NZ + len(stores)]))
        stores[-1].start()

    for k in range(PANELS):
        for j in range(SLOTS):
            keep(up.at[k, j], r_out.at[k, :, j, :])
    for each in stores:
        each.wait()

    @pl.loop(0, 2 * NZ)
    def _(n):
        for i, (j, lanes) in enumerate(blocks(n)):
            store(n, i, j, lanes).wait()

    for k in range(PANELS):
        relay[k].drain()
        gather[k].drain()

    @pl.when(x == 0)
    def _():
        whole[0].drain_sums()
        for copies in across:
            drain(copies)

    whole[0].drain_shares()
    whole[1].drain()
    whole[2].drain()
    scatter[1].drain()


def on_device(matrix):
    n = matrix.shape[0]
    scale = float(n * lax.axis_size("row")) ** 0.5
    dma = pltpu.SemaphoreType.DMA

    def vmem(*dims):
        return pltpu.VMEM(dims, F32)

    share = W // lax.axis_size("row")
    square = vmem(W, W)
    return pl.pallas_call(
        functools.partial(kernel, scale),
        out_shape=(
            jax.ShapeDtypeStruct((n, SLOTS, W), F32), jax.ShapeDtypeStruct((PANELS, share, SLOTS, W), F32),
        ),
        in_specs=[ANY],
        out_specs=(ANY, ANY),
        scratch_shapes=[
            vmem(SLOTS, n, W), vmem(n, W), vmem(n, W), vmem(n, W), vmem(n, W), vmem(n, W), square, square, square, square,
            square, vmem(8, LEAF), vmem(3, W, W), vmem(3, W, W), vmem(3, W // 2, W), vmem(3, 2, 3, 32, W), vmem(3, 2, 3, 8, W),
            vmem(SLOTS, W, W), vmem(2, 2, W, W), vmem(2, 2, 3, 128, W), vmem(2, 2, 3, 32, W), vmem(2, SLOTS, W, W),
            vmem(PANELS, SLOTS, share, W), vmem(2, 32, W), pltpu.VMEM((2, W + share, W), jnp.bfloat16),
            pltpu.VMEM((2, W + share, W), jnp.bfloat16), dma((208,)), dma((208,)), dma((32,)),
        ],
        compiler_params=pltpu.CompilerParams(
            collective_id=1, has_side_effects=True, vmem_limit_bytes=63 * 2**20
        ),
        name="qr",
    )(matrix)


def solution(mesh):
    return jax.shard_map(
        on_device,
        mesh=mesh,
        in_specs=(P("row", "col", None),),
        out_specs=(P("row", "col", None), P(None, "row", "col", None)),
        check_vma=False,
    )
```
